512 devices in a mesh: row: 32 (over z, x_lo, core), col: 16 (over x_hi, y).
Axes of the slice: x: 4 (x_hi: 2, x_lo: 2; x = x_hi * 2 + x_lo), y: 8, z: 8, core: 2. Of those that a mesh axis runs over, the one named last changes fastest.
Arguments:
- grm_prior: float32 [4096, 4096], P('row', 'col'), may hold values from -0.6 to 0.6
- dosage_now: bfloat16 [4096, 4096], P('row', 'col'), may hold values from 0 to 2
- mask_now: int32 [4096, 4096], P('row', 'col'), may hold values 0 or 1
- dosage_prev: bfloat16 [4096, 256], P('row'), may hold values from 0 to 2
- mask_prev: int32 [4096, 256], P('row'), may hold values 0 or 1
- expression: bfloat16 [4096, 20480], P('row', 'col'), may hold values from -18 to 18
Outputs:
- grm_total: float32 [4096, 4096], P('row', 'col')
- assoc_score: float32 [256, 20480], P('row', 'col')
The draws below stay inside these ranges and needn't reach their ends.
All inputs are finite; a program needn't handle non-finite values. No bound on the sum of `mask_now` or of `mask_prev` on one device may be relied on, other than what follows from the above.
Results may differ from the reference program's by a relative error of at most 0.0029.
Values may be sent and summed in bfloat16 or wider, within the bound.
No kernel may reach another device: no remote copies, remote signals or barrier semaphores. Data moves between devices by JAX's collectives and lax.ppermute only.
A program may use at most 64 MiB of HBM per device.

```python
import math
import jax
import jax.numpy as jnp
from jax import lax

VARIANTS = 4096
ASSOC_VAR = 256
GENES = 20480
SAMPLES = 4096


def make_dosage(key, width):
    freq_key, draw_key = jax.random.split(key, 2)
    sample_ramp = (1.0 + 2.0 * jnp.arange(SAMPLES, dtype=jnp.float32) / (SAMPLES - 1)) / 3.0
    allele = jax.random.uniform(freq_key, (1, width), jnp.float32, 0.1, 0.5)
    base_draw = jax.random.uniform(draw_key, (SAMPLES, width), jnp.float32)
    return (4.0 * allele * base_draw * sample_ramp[:, None]).astype(jnp.bfloat16)


def draw_dosage_now(key, part):
    return make_dosage(jax.random.fold_in(key, 11), VARIANTS)


def draw_dosage_prev(key, part):
    return make_dosage(jax.random.fold_in(key, 23), ASSOC_VAR)


def draw_expression(key, part):
    inner_key = jax.random.fold_in(key, 37)
    noise_key = jax.random.fold_in(inner_key, 0)
    sample_ramp = 1.0 + 2.0 * jnp.arange(SAMPLES, dtype=jnp.float32) / (SAMPLES - 1)
    values = jnp.clip(jax.random.normal(noise_key, (SAMPLES, GENES), jnp.float32), -6.0, 6.0)
    return (values * sample_ramp[:, None]).astype(jnp.bfloat16)


def place_ends(array, rng, smallest, largest):
    longest = array.shape.index(max(array.shape))
    spots = []
    for shift in (0, 1):
        where = [jax.random.randint(jax.random.fold_in(rng, axis), (), 0, length) for axis, length in enumerate(array.shape)]
        where[longest] = (where[longest] + shift) % array.shape[longest]
        spots.append(tuple(where))
    return array.at[spots[0]].set(smallest).at[spots[1]].set(largest)


def levels(own_key, extent, cuts, low, largest):
    gain, own = 1.0, jax.random.fold_in(own_key, 6)
    for dim, blocks in cuts:
        steps = jnp.exp(jax.random.uniform(jax.random.fold_in(own, dim), (blocks,), jnp.float32, low / len(cuts), largest / len(cuts)))
        gain = gain * jnp.repeat(steps, extent[dim] // blocks).reshape([-1 if axis == dim else 1 for axis in range(len(extent))])
    return gain


def gaussian(own_key, extent, scale, reach, cuts=(), kind=jnp.bfloat16):
    values = scale * jax.random.normal(own_key, extent, jnp.float32)
    if cuts:
        values = values * levels(own_key, extent, cuts, -0.22, 0.18)
    return jnp.clip(values, -reach, reach).astype(kind)


def setup_inputs(seed: int = 0) -> dict:
    key_list = jax.random.split(jax.random.key(seed), 7)
    grm_prior = gaussian(key_list[0], (SAMPLES, SAMPLES), 0.1, 0.6, ((0, 32), (1, 16)), jnp.float32)
    dosage_now = draw_dosage_now(jax.random.fold_in(key_list[6], 71), 0)
    mask_now = place_ends((jax.random.randint(key_list[2], (SAMPLES, VARIANTS), 0, 10) < 9).astype(jnp.int32), jax.random.fold_in(key_list[2], 1), 0, 1)
    dosage_prev = draw_dosage_prev(jax.random.fold_in(key_list[6], 71), 0)
    mask_prev = place_ends((jax.random.randint(key_list[4], (SAMPLES, ASSOC_VAR), 0, 10) < 9).astype(jnp.int32), jax.random.fold_in(key_list[4], 1), 0, 1)
    expression = draw_expression(jax.random.fold_in(key_list[6], 71), 0)
    return dict(grm_prior=grm_prior, dosage_now=dosage_now, mask_now=mask_now, dosage_prev=dosage_prev, mask_prev=mask_prev, expression=expression)


epsilon = 1e-05

def moments(dosage, present):
    values = dosage.astype(jnp.float32)
    weight = present.astype(jnp.float32)
    observed = jnp.maximum(lax.optimization_barrier(jnp.sum(weight, 0)), 1.0)
    centre = lax.optimization_barrier(jnp.sum(weight * values, 0)) / observed
    offset = weight * (values - centre)
    spread = lax.optimization_barrier(jnp.sum(offset * offset, 0)) / observed
    return (offset, spread)

def reference(grm_prior, dosage_now, mask_now, dosage_prev, mask_prev, expression):
    offset_now, spread_now = moments(dosage_now, mask_now)
    scaled = (offset_now * lax.rsqrt(spread_now + epsilon)).astype(jnp.bfloat16)
    wide = scaled.astype(jnp.float32)
    product = jnp.dot(wide, wide.T, precision=lax.Precision.HIGHEST, preferred_element_type=jnp.float32)
    grm_total = grm_prior + product / VARIANTS
    offset_prev, spread_prev = moments(dosage_prev, mask_prev)
    genotype = offset_prev.astype(jnp.bfloat16).astype(jnp.float32)
    traits = expression.astype(jnp.float32)
    cross_sum = lax.dot_general(genotype, traits, (((0,), (0,)), ((), ())), precision=lax.Precision.HIGHEST, preferred_element_type=jnp.float32)
    power = lax.optimization_barrier(jnp.sum(traits * traits, 0)) / SAMPLES
    assoc_score = cross_sum * lax.rsqrt(spread_prev + epsilon)[:, None] * lax.rsqrt(power + epsilon)[None, :] / math.sqrt(SAMPLES)
    return (grm_total, assoc_score)
```

```python
import math

import jax
import jax.numpy as jnp
from jax import lax
from jax.sharding import PartitionSpec as P

VARIANTS = 4096
epsilon = 1e-05
EVERY = ("row", "col")
CORES = 2


def local_moments(dosage, present):
    values = dosage.astype(jnp.float32)
    weight = present.astype(jnp.float32)
    kept = weight * values
    return jnp.stack([jnp.sum(weight, 0), jnp.sum(kept, 0), jnp.sum(kept * values, 0)])


def summed_over_rows(flat):
    peers = lax.axis_size("row")
    sent = jnp.broadcast_to(flat[None, None], (peers, 1, flat.size))
    return jnp.sum(lax.all_to_all(sent, "row", 0, 0, tiled=True), axis=(0, 1))


def finished(moments):
    seen, summed, raw = moments
    observed = jnp.maximum(seen, 1.0)
    centre = summed / observed
    return centre, raw / observed - centre * centre


def half_of(stacked, bit, axis=0):
    return lax.dynamic_index_in_dim(stacked, bit, axis, keepdims=False)


def folded(stacked, bit, pairs):
    arrived = lax.ppermute(half_of(stacked, 1 - bit), EVERY, pairs)
    return half_of(stacked, bit) + arrived


def body(grm_prior, dosage_now, mask_now, dosage_prev, mask_prev, expression):
    rows, cols = lax.axis_size("row"), lax.axis_size("col")
    chips = rows // CORES
    row, col = lax.axis_index("row"), lax.axis_index("col")
    core = row % CORES
    samples_all = dosage_now.shape[0] * rows
    width = dosage_now.shape[1]
    tested = dosage_prev.shape[1]

    def at(chip, half, column):
        return (chip * CORES + half) * cols + column

    blocks = [(k, c) for k in range(chips) for c in range(cols)]

    traits = expression.astype(jnp.float32)
    moments_now = local_moments(dosage_now, mask_now)
    moments_prev = local_moments(dosage_prev, mask_prev)
    squares = jnp.sum(traits * traits, 0)
    total = summed_over_rows(
        jnp.concatenate([moments_now.reshape(-1), moments_prev.reshape(-1), squares])
    )
    centre_now, spread_now = finished(total[: 3 * width].reshape(3, width))
    centre_prev, spread_prev = finished(
        total[3 * width : 3 * (width + tested)].reshape(3, tested)
    )
    squares = total[3 * (width + tested) :]

    weight_now = mask_now.astype(jnp.float32)
    scaled = (
        weight_now * (dosage_now.astype(jnp.float32) - centre_now)
        * lax.rsqrt(spread_now + epsilon)
    ).astype(jnp.bfloat16)
    crossed = lax.ppermute(
        scaled,
        EVERY,
        [(at(k, 1, c), at(k, 0, c)) for k, c in blocks]
        + [(at(c, 0, k), at(k, 1, c)) for k, c in blocks],
    )
    mirrored = lax.ppermute(
        scaled, EVERY, [(at(c, 1, k), at(k, 1, c)) for k, c in blocks]
    )
    first = core == 0
    chip_block = jnp.stack(
        [jnp.where(first, scaled, crossed), jnp.where(first, crossed, mirrored)]
    )
    groups = [[at(k, 0, c) for c in range(cols)] for k in range(chips)] + [
        [at(k, 1, c) for k in range(chips)] for c in range(cols)
    ]
    panel = lax.all_to_all(
        jnp.broadcast_to(chip_block[None], (cols, *chip_block.shape)),
        EVERY,
        0,
        0,
        tiled=True,
        axis_index_groups=groups,
    )

    weight_prev = mask_prev.astype(jnp.float32)
    genotype = (weight_prev * (dosage_prev.astype(jnp.float32) - centre_prev)).astype(jnp.bfloat16)
    cross = lax.dot_general(
        genotype, expression, (((0,), (0,)), ((), ())), preferred_element_type=jnp.float32
    )
    out_rows = tested // rows
    genes = expression.shape[1]
    cross = cross.reshape(chips, CORES, out_rows, genes)
    cross = folded(
        jnp.moveaxis(cross, 1, 0),
        core,
        [(at(k, h, c), at(k, 1 - h, c)) for k, c in blocks for h in range(CORES)],
    )
    chip = row // CORES
    span = 1
    while span < chips:
        bit = (chip // span) % 2
        cross = folded(
            jnp.moveaxis(cross.reshape(-1, 2, out_rows, genes), 1, 0),
            bit,
            [(at(k, h, c), at(k ^ span, h, c)) for k, c in blocks for h in range(CORES)],
        )
        span *= 2
    cross = cross.reshape(out_rows, genes)
    spread_rows = lax.dynamic_slice_in_dim(spread_prev, row * out_rows, out_rows, 0)
    power = squares / samples_all
    assoc_score = (
        cross
        * lax.rsqrt(spread_rows + epsilon)[:, None]
        * lax.rsqrt(power + epsilon)[None, :]
        / math.sqrt(samples_all)
    )

    upper, lower = panel[:, 0], panel[:, 1]
    swap = [(at(k, h, c), at(k, 1 - h, c)) for k, c in blocks for h in range(CORES)]
    other = lax.ppermute(jnp.where(first, lower, upper), EVERY, swap)
    rest = lax.ppermute(lower, EVERY, [(at(k, 1, c), at(k, 0, c)) for k, c in blocks])

    def product(a, b):
        return lax.dot_general(
            a, b, (((0, 2), (0, 2)), ((), ())), preferred_element_type=jnp.float32
        )

    mine = jnp.where(first, upper, other)
    left = product(mine, jnp.where(first, other, upper))
    right = product(mine, jnp.where(first, rest, lower))
    grm_total = grm_prior + jnp.concatenate([left, right], 1) / VARIANTS
    return (grm_total, assoc_score)


def solution(mesh):
    assert mesh.shape["row"] == CORES * mesh.shape["col"]
    in_specs = (
        P("row", "col"),
        P("row", "col"),
        P("row", "col"),
        P("row", None),
        P("row", None),
        P("row", "col"),
    )
    out_specs = (P("row", "col"), P("row", "col"))
    return jax.shard_map(body, mesh=mesh, in_specs=in_specs, out_specs=out_specs, check_vma=False)
```

```python
import math

import jax
import jax.numpy as jnp
from jax import lax
from jax.sharding import PartitionSpec as P

VARIANTS = 4096
epsilon = 1e-05
EVERY = ("row", "col")
CORES = 2


def local_moments(dosage, present):
    values = dosage.astype(jnp.float32)
    weight = present.astype(jnp.float32)
    kept = weight * values
    return jnp.stack([jnp.sum(weight, 0), jnp.sum(kept, 0), jnp.sum(kept * values, 0)])


def summed_over(flat, groups):
    peers = len(groups[0])
    sent = jnp.broadcast_to(flat[None, None], (peers, 1, flat.size))
    arrived = lax.all_to_all(sent, EVERY, 0, 0, tiled=True, axis_index_groups=groups)
    return jnp.sum(arrived, axis=(0, 1))


def finished(moments):
    seen, summed, raw = moments
    observed = jnp.maximum(seen, 1.0)
    centre = summed / observed
    return centre, raw / observed - centre * centre


def half_of(stacked, bit, axis=0):
    return lax.dynamic_index_in_dim(stacked, bit, axis, keepdims=False)


def folded(stacked, bit, pairs):
    leaving = half_of(stacked, 1 - bit).astype(jnp.bfloat16)
    return half_of(stacked, bit) + lax.ppermute(leaving, EVERY, pairs).astype(jnp.float32)


def body(grm_prior, dosage_now, mask_now, dosage_prev, mask_prev, expression):
    rows, cols = lax.axis_size("row"), lax.axis_size("col")
    chips = rows // CORES
    row, col = lax.axis_index("row"), lax.axis_index("col")
    core = row % CORES
    samples_all = dosage_now.shape[0] * rows
    width = dosage_now.shape[1]
    tested = dosage_prev.shape[1]

    def at(chip, half, column):
        return (chip * CORES + half) * cols + column

    blocks = [(k, c) for k in range(chips) for c in range(cols)]

    traits = expression.astype(jnp.float32)
    moments_now = local_moments(dosage_now, mask_now)
    moments_prev = local_moments(dosage_prev, mask_prev)
    squares = jnp.sum(traits * traits, 0)
    swap = [(at(k, h, c), at(k, 1 - h, c)) for k, c in blocks for h in range(CORES)]
    partial = jnp.concatenate([moments_now.reshape(-1), moments_prev.reshape(-1), squares])
    partial = partial + lax.ppermute(partial, EVERY, swap)
    columns = [[at(k, h, c) for k in range(chips)] for c in range(cols) for h in range(CORES)]
    total = summed_over(partial, columns)
    centre_now, spread_now = finished(total[: 3 * width].reshape(3, width))
    centre_prev, spread_prev = finished(
        total[3 * width : 3 * (width + tested)].reshape(3, tested)
    )
    squares = total[3 * (width + tested) :]

    weight_now = mask_now.astype(jnp.float32)
    scaled = (
        weight_now * (dosage_now.astype(jnp.float32) - centre_now)
        * lax.rsqrt(spread_now + epsilon)
    ).astype(jnp.bfloat16)
    crossed = lax.ppermute(
        scaled,
        EVERY,
        [(at(k, 1, c), at(k, 0, c)) for k, c in blocks]
        + [(at(c, 0, k), at(k, 1, c)) for k, c in blocks],
    )
    mirrored = lax.ppermute(
        scaled, EVERY, [(at(c, 1, k), at(k, 1, c)) for k, c in blocks]
    )
    weight_prev = mask_prev.astype(jnp.float32)
    genotype = (weight_prev * (dosage_prev.astype(jnp.float32) - centre_prev)).astype(jnp.bfloat16)
    cross = lax.dot_general(
        genotype, expression, (((0,), (0,)), ((), ())), preferred_element_type=jnp.float32
    )
    out_rows = tested // rows
    genes = expression.shape[1]
    layers = chips // 2
    chip = row // CORES
    level, side = chip // 2, chip % 2
    near = layers // 2
    cross = cross.reshape(layers, 2, CORES * out_rows, genes)
    cross = jnp.concatenate([cross, cross], 0)
    above = lax.dynamic_slice_in_dim(cross, level + 1, near, 0)
    below = lax.dynamic_slice_in_dim(cross, level + 1 + near, near, 0)
    first = core == 0
    leaving = jnp.where(first, below, above).astype(jnp.bfloat16)
    cross = jnp.where(first, above, below) + lax.ppermute(leaving, EVERY, swap).astype(jnp.float32)
    cross = folded(
        jnp.moveaxis(cross, 1, 0),
        side,
        [(at(k, h, c), at(k ^ 1, h, c)) for k, c in blocks for h in range(CORES)],
    )
    chip_block = jnp.stack(
        [jnp.where(first, scaled, crossed), jnp.where(first, crossed, mirrored)]
    )
    groups = [[at(k, 0, c) for c in range(cols)] for k in range(chips)] + [
        [at(k, 1, c) for k in range(chips)] for c in range(cols)
    ]
    chip_block, cross = lax.optimization_barrier((chip_block, cross))
    panel = lax.all_to_all(
        jnp.broadcast_to(chip_block[None], (cols, *chip_block.shape)),
        EVERY,
        0,
        0,
        tiled=True,
        axis_index_groups=groups,
    )

    wire = cross.astype(jnp.bfloat16)
    total_rows = jnp.where(first, 0.0, cross[near - 1])
    for far in range(1, near + 1):
        upward = [(at(k, 0, c), at((k + 2 * far) % chips, 0, c)) for k, c in blocks]
        downward = [(at(k, 1, c), at((k - 2 * far) % chips, 1, c)) for k, c in blocks]
        if far < near:
            leaving = jnp.where(first, wire[far - 1], wire[near - 1 - far])
            arrived = lax.ppermute(leaving, EVERY, upward + downward)
        else:
            arrived = lax.ppermute(wire[far - 1], EVERY, upward)
        total_rows = total_rows + arrived.astype(jnp.float32)
    shares = total_rows.reshape(CORES, out_rows, genes)
    cross = half_of(shares, core) + lax.ppermute(half_of(shares, 1 - core), EVERY, swap)
    spread_rows = lax.dynamic_slice_in_dim(spread_prev, row * out_rows, out_rows, 0)
    power = squares / samples_all
    assoc_score = (
        cross
        * lax.rsqrt(spread_rows + epsilon)[:, None]
        * lax.rsqrt(power + epsilon)[None, :]
        / math.sqrt(samples_all)
    )

    upper, lower = panel[:, 0], panel[:, 1]
    other = lax.ppermute(jnp.where(first, lower, upper), EVERY, swap)
    rest = lax.ppermute(lower, EVERY, [(at(k, 1, c), at(k, 0, c)) for k, c in blocks])

    def product(a, b):
        return lax.dot_general(
            a, b, (((0, 2), (0, 2)), ((), ())), preferred_element_type=jnp.float32
        )

    mine = jnp.where(first, upper, other)
    left = product(mine, jnp.where(first, other, upper))
    right = product(mine, jnp.where(first, rest, lower))
    grm_total = grm_prior + jnp.concatenate([left, right], 1) / VARIANTS
    return (grm_total, assoc_score)


def solution(mesh):
    assert mesh.shape["row"] == CORES * mesh.shape["col"]
    in_specs = (
        P("row", "col"),
        P("row", "col"),
        P("row", "col"),
        P("row", None),
        P("row", None),
        P("row", "col"),
    )
    out_specs = (P("row", "col"), P("row", "col"))
    return jax.shard_map(body, mesh=mesh, in_specs=in_specs, out_specs=out_specs, check_vma=False)
```

```python
import math

import jax
import jax.numpy as jnp
from jax import lax
from jax.sharding import PartitionSpec as P

VARIANTS = 4096
epsilon = 1e-05
EVERY = ("row", "col")
CORES = 2


def local_moments(dosage, present):
    values = dosage.astype(jnp.float32)
    weight = present.astype(jnp.float32)
    kept = weight * values
    return jnp.stack([jnp.sum(weight, 0), jnp.sum(kept, 0), jnp.sum(kept * values, 0)])


def summed_over(flat, groups):
    peers = len(groups[0])
    sent = jnp.broadcast_to(flat[None, None], (peers, 1, flat.size))
    arrived = lax.all_to_all(sent, EVERY, 0, 0, tiled=True, axis_index_groups=groups)
    return jnp.sum(arrived, axis=(0, 1))


def finished(moments):
    seen, summed, raw = moments
    observed = jnp.maximum(seen, 1.0)
    centre = summed / observed
    return centre, raw / observed - centre * centre


def half_of(stacked, bit, axis=0):
    return lax.dynamic_index_in_dim(stacked, bit, axis, keepdims=False)


def folded(stacked, bit, pairs):
    return half_of(stacked, bit) + lax.ppermute(half_of(stacked, 1 - bit), EVERY, pairs)


def landing(chips, cols):
    sides, tall, wide = 2, chips // 2, cols // 2
    steps = sorted(range(wide), key=lambda d: min(d, wide - d))
    climbs = sorted(range(tall), key=lambda d: -min(d, tall - d))
    table = []
    for c in range(cols):
        z, low, high, y = c // sides, c % sides, c // wide, c % wide
        targets = [0] * cols
        for step, climb in zip(steps, climbs):
            sources = [half * wide + (y + step) % wide for half in range(2)]
            ends = [(z + climb) % tall * sides + side for side in range(sides)]

            def reach(source, end):
                gap = (source // wide * 2 + low - high * 2 - end % sides) % 4
                return min(gap, 4 - gap)

            straight = [reach(sources[i], ends[i]) for i in range(2)]
            turned = [reach(sources[i], ends[1 - i]) for i in range(2)]
            if max(turned) < max(straight):
                ends = ends[::-1]
            for source, end in zip(sources, ends):
                targets[source] = end
        table.append(targets)
    return table


def body(grm_prior, dosage_now, mask_now, dosage_prev, mask_prev, expression):
    rows, cols = lax.axis_size("row"), lax.axis_size("col")
    chips = rows // CORES
    row, col = lax.axis_index("row"), lax.axis_index("col")
    core = row % CORES
    samples_all = dosage_now.shape[0] * rows
    width = dosage_now.shape[1]
    tested = dosage_prev.shape[1]

    def at(chip, half, column):
        return (chip * CORES + half) * cols + column

    lands = landing(chips, cols)
    blocks = [(k, c) for k in range(chips) for c in range(cols)]

    traits = expression.astype(jnp.float32)
    moments_now = local_moments(dosage_now, mask_now)
    moments_prev = local_moments(dosage_prev, mask_prev)
    squares = jnp.sum(traits * traits, 0)
    swap = [(at(k, h, c), at(k, 1 - h, c)) for k, c in blocks for h in range(CORES)]
    partial = jnp.concatenate([moments_now.reshape(-1), moments_prev.reshape(-1), squares])
    partial = partial + lax.ppermute(partial, EVERY, swap)
    columns = [[at(k, h, c) for k in range(chips)] for c in range(cols) for h in range(CORES)]
    total = summed_over(partial, columns)
    centre_now, spread_now = finished(total[: 3 * width].reshape(3, width))
    centre_prev, spread_prev = finished(
        total[3 * width : 3 * (width + tested)].reshape(3, tested)
    )
    squares = total[3 * (width + tested) :]

    chip = row // CORES
    level, side = chip // 2, chip % 2
    across = [(at(k, h, c), at(k ^ 1, h, c)) for k, c in blocks for h in range(CORES)]
    genes = expression.shape[1]
    share = genes // 2
    halves = expression.reshape(-1, 2, share)
    weight_prev = mask_prev.astype(jnp.bfloat16)
    tested_raw = [weight_prev * dosage_prev, weight_prev]
    raw = jnp.concatenate([half_of(halves, 1 - side, 1), *tested_raw], 1)
    held = jnp.concatenate([half_of(halves, side, 1), *tested_raw], 1)
    held = jnp.concatenate([held, lax.ppermute(raw, EVERY, across)], 0)
    held = jnp.concatenate([held, lax.ppermute(held, EVERY, swap)], 0)

    weight_now = mask_now.astype(jnp.float32)
    scaled = (
        weight_now * (dosage_now.astype(jnp.float32) - centre_now)
        * lax.rsqrt(spread_now + epsilon)
    ).astype(jnp.bfloat16)
    crossed = lax.ppermute(
        scaled,
        EVERY,
        [(at(k, 1, c), at(k, 0, c)) for k, c in blocks]
        + [(at(c, 0, v), at(lands[c][v], 1, c)) for c, v in blocks],
    )
    mirrored = lax.ppermute(
        scaled, EVERY, [(at(c, 1, v), at(lands[c][v], 1, c)) for c, v in blocks]
    )
    genotype = (
        held[:, share + tested :].astype(jnp.float32)
        * (held[:, share : share + tested].astype(jnp.float32) - centre_prev)
    ).astype(jnp.bfloat16)
    layers = chips // 2
    near = layers // 2
    out_rows = tested // rows
    cross = lax.dot_general(
        genotype, held[:, :share], (((0,), (0,)), ((), ())), preferred_element_type=jnp.float32
    ).reshape(layers, 2 * CORES * out_rows, share)
    first = core == 0
    chip_block = jnp.stack(
        [jnp.where(first, scaled, crossed), jnp.where(first, crossed, mirrored)]
    )
    groups = [[at(k, 0, c) for c in range(cols)] for k in range(chips)] + [
        [at(k, 1, c) for k in lands[c]] for c in range(cols)
    ]
    chip_block, cross = lax.optimization_barrier((chip_block, cross))
    panel = lax.all_to_all(
        jnp.broadcast_to(chip_block[None], (cols, *chip_block.shape)),
        EVERY,
        0,
        0,
        tiled=True,
        axis_index_groups=groups,
    )

    kept = jnp.where(first, 0.0, lax.dynamic_index_in_dim(cross, level, 0, keepdims=False))
    arrivals = []
    for far in range(1, near + 1):
        routes = [(at(k, 0, c), at((k + 2 * far) % chips, 0, c)) for k, c in blocks]
        goal = (level + far) % layers
        if far < near:
            routes += [(at(k, 1, c), at((k - 2 * far) % chips, 1, c)) for k, c in blocks]
            goal = jnp.where(first, goal, (level + layers - far) % layers)
        leaving = lax.dynamic_index_in_dim(cross, goal, 0, keepdims=False)
        arrivals.append(lax.ppermute(leaving, EVERY, routes))

    upper, lower = panel[:, 0], panel[:, 1]
    leaving, kept = lax.optimization_barrier((jnp.where(first, lower, upper), kept))
    other = lax.ppermute(leaving, EVERY, swap)
    rest = lax.ppermute(lower, EVERY, [(at(k, 1, c), at(k, 0, c)) for k, c in blocks])

    total_rows = kept
    for arrived in arrivals:
        total_rows = total_rows + arrived
    shares = folded(
        jnp.moveaxis(total_rows.reshape(2, CORES, out_rows, share), 1, 0), core, swap
    )
    own, other_half = half_of(shares, side), lax.ppermute(half_of(shares, 1 - side), EVERY, across)
    left_chip = side == 0
    cross = jnp.concatenate(
        [jnp.where(left_chip, own, other_half), jnp.where(left_chip, other_half, own)], 1
    )
    spread_rows = lax.dynamic_slice_in_dim(spread_prev, row * out_rows, out_rows, 0)
    power = squares / samples_all
    assoc_score = (
        cross
        * lax.rsqrt(spread_rows + epsilon)[:, None]
        * lax.rsqrt(power + epsilon)[None, :]
        / math.sqrt(samples_all)
    )

    def product(a, b):
        return lax.dot_general(
            a, b, (((0, 2), (0, 2)), ((), ())), preferred_element_type=jnp.float32
        )

    mine = jnp.where(first, upper, other)
    left = product(mine, jnp.where(first, other, upper))
    right = product(mine, jnp.where(first, rest, lower))
    grm_total = grm_prior + jnp.concatenate([left, right], 1) / VARIANTS
    return (grm_total, assoc_score)


def solution(mesh):
    assert mesh.shape["row"] == CORES * mesh.shape["col"]
    in_specs = (
        P("row", "col"),
        P("row", "col"),
        P("row", "col"),
        P("row", None),
        P("row", None),
        P("row", "col"),
    )
    out_specs = (P("row", "col"), P("row", "col"))
    return jax.shard_map(body, mesh=mesh, in_specs=in_specs, out_specs=out_specs, check_vma=False)
```

```python
import math

import jax
import jax.numpy as jnp
from jax import lax
from jax.sharding import PartitionSpec as P

VARIANTS = 4096
epsilon = 1e-05
EVERY = ("row", "col")
CORES = 2


def local_moments(dosage, present):
    values = dosage.astype(jnp.float32)
    weight = present.astype(jnp.float32)
    kept = weight * values
    return jnp.stack([jnp.sum(weight, 0), jnp.sum(kept, 0), jnp.sum(kept * values, 0)])


def summed_over(flat, groups):
    peers = len(groups[0])
    sent = jnp.broadcast_to(flat[None, None], (peers, 1, flat.size))
    arrived = lax.all_to_all(sent, EVERY, 0, 0, tiled=True, axis_index_groups=groups)
    return jnp.sum(arrived, axis=(0, 1))


def finished(moments):
    seen, summed, raw = moments
    observed = jnp.maximum(seen, 1.0)
    centre = summed / observed
    return centre, raw / observed - centre * centre


def half_of(stacked, bit, axis=0):
    return lax.dynamic_index_in_dim(stacked, bit, axis, keepdims=False)


def folded(stacked, bit, pairs):
    return half_of(stacked, bit) + lax.ppermute(half_of(stacked, 1 - bit), EVERY, pairs)


def landing(chips, cols):
    sides, tall, wide = 2, chips // 2, cols // 2
    steps = sorted(range(wide), key=lambda d: min(d, wide - d))
    climbs = sorted(range(tall), key=lambda d: -min(d, tall - d))
    table = []
    for c in range(cols):
        z, low, high, y = c // sides, c % sides, c // wide, c % wide
        targets = [0] * cols
        for step, climb in zip(steps, climbs):
            sources = [half * wide + (y + step) % wide for half in range(2)]
            ends = [(z + climb) % tall * sides + side for side in range(sides)]

            def reach(source, end):
                gap = (source // wide * 2 + low - high * 2 - end % sides) % 4
                return min(gap, 4 - gap)

            straight = [reach(sources[i], ends[i]) for i in range(2)]
            turned = [reach(sources[i], ends[1 - i]) for i in range(2)]
            if max(turned) < max(straight):
                ends = ends[::-1]
            for source, end in zip(sources, ends):
                targets[source] = end
        table.append(targets)
    return table


def body(grm_prior, dosage_now, mask_now, dosage_prev, mask_prev, expression):
    rows, cols = lax.axis_size("row"), lax.axis_size("col")
    chips = rows // CORES
    row, col = lax.axis_index("row"), lax.axis_index("col")
    core = row % CORES
    samples_all = dosage_now.shape[0] * rows
    width = dosage_now.shape[1]
    tested = dosage_prev.shape[1]

    def at(chip, half, column):
        return (chip * CORES + half) * cols + column

    lands = landing(chips, cols)
    blocks = [(k, c) for k in range(chips) for c in range(cols)]

    traits = expression.astype(jnp.float32)
    moments_now = local_moments(dosage_now, mask_now)
    moments_prev = local_moments(dosage_prev, mask_prev)
    squares = jnp.sum(traits * traits, 0)
    swap = [(at(k, h, c), at(k, 1 - h, c)) for k, c in blocks for h in range(CORES)]
    partial = jnp.concatenate([moments_now.reshape(-1), moments_prev.reshape(-1), squares])
    partial = partial + lax.ppermute(partial, EVERY, swap)
    columns = [[at(k, h, c) for k in range(chips)] for c in range(cols) for h in range(CORES)]
    total = summed_over(partial, columns)
    centre_now, spread_now = finished(total[: 3 * width].reshape(3, width))
    centre_prev, spread_prev = finished(
        total[3 * width : 3 * (width + tested)].reshape(3, tested)
    )
    squares = total[3 * (width + tested) :]

    first = core == 0
    weight_now = mask_now.astype(jnp.bfloat16)
    kept_now = weight_now * dosage_now
    pair_now = lax.ppermute(jnp.stack([kept_now, weight_now]), EVERY, swap)

    chip = row // CORES
    level, side = chip // 2, chip % 2
    across = [(at(k, h, c), at(k ^ 1, h, c)) for k, c in blocks for h in range(CORES)]
    genes = expression.shape[1]
    share = genes // 2
    halves = expression.reshape(-1, 2, share)
    weight_prev = mask_prev.astype(jnp.bfloat16)
    tested_raw = [weight_prev * dosage_prev, weight_prev]
    raw = jnp.concatenate([half_of(halves, 1 - side, 1), *tested_raw], 1)
    held = jnp.concatenate([half_of(halves, side, 1), *tested_raw], 1)
    held = jnp.concatenate([held, lax.ppermute(raw, EVERY, across)], 0)
    held = jnp.concatenate([held, lax.ppermute(held, EVERY, swap)], 0)

    def standardized(kept, weight):
        offset = weight.astype(jnp.float32) * (kept.astype(jnp.float32) - centre_now)
        return (offset * lax.rsqrt(spread_now + epsilon)).astype(jnp.bfloat16)

    mine = standardized(kept_now, weight_now)
    partner = standardized(pair_now[0], pair_now[1])
    chip_block = jnp.stack(
        [jnp.where(first, mine, partner), jnp.where(first, partner, mine)]
    )
    mirrored = lax.ppermute(
        chip_block, EVERY, [(at(c, 1, v), at(lands[c][v], 1, c)) for c, v in blocks]
    )
    chip_block = jnp.where(first, chip_block, mirrored)
    genotype = (
        held[:, share + tested :].astype(jnp.float32)
        * (held[:, share : share + tested].astype(jnp.float32) - centre_prev)
    ).astype(jnp.bfloat16)
    layers = chips // 2
    near = layers // 2
    out_rows = tested // rows
    cross = lax.dot_general(
        genotype, held[:, :share], (((0,), (0,)), ((), ())), preferred_element_type=jnp.float32
    ).reshape(layers, 2 * CORES * out_rows, share)
    groups = [[at(k, 0, c) for c in range(cols)] for k in range(chips)] + [
        [at(k, 1, c) for k in lands[c]] for c in range(cols)
    ]
    chip_block, cross = lax.optimization_barrier((chip_block, cross))
    panel = lax.all_to_all(
        jnp.broadcast_to(chip_block[None], (cols, *chip_block.shape)),
        EVERY,
        0,
        0,
        tiled=True,
        axis_index_groups=groups,
    )

    kept = jnp.where(first, 0.0, lax.dynamic_index_in_dim(cross, level, 0, keepdims=False))
    arrivals = []
    for far in range(1, near + 1):
        routes = [(at(k, 0, c), at((k + 2 * far) % chips, 0, c)) for k, c in blocks]
        goal = (level + far) % layers
        if far < near:
            routes += [(at(k, 1, c), at((k - 2 * far) % chips, 1, c)) for k, c in blocks]
            goal = jnp.where(first, goal, (level + layers - far) % layers)
        leaving = lax.dynamic_index_in_dim(cross, goal, 0, keepdims=False)
        arrivals.append(lax.ppermute(leaving, EVERY, routes))

    upper, lower = panel[:, 0], panel[:, 1]
    leaving, kept = lax.optimization_barrier((jnp.where(first, lower, upper), kept))
    other = lax.ppermute(leaving, EVERY, swap)
    rest = lax.ppermute(lower, EVERY, [(at(k, 1, c), at(k, 0, c)) for k, c in blocks])

    total_rows = kept
    for arrived in arrivals:
        total_rows = total_rows + arrived
    shares = folded(
        jnp.moveaxis(total_rows.reshape(2, CORES, out_rows, share), 1, 0), core, swap
    )
    own, other_half = half_of(shares, side), lax.ppermute(half_of(shares, 1 - side), EVERY, across)
    left_chip = side == 0
    cross = jnp.concatenate(
        [jnp.where(left_chip, own, other_half), jnp.where(left_chip, other_half, own)], 1
    )
    spread_rows = lax.dynamic_slice_in_dim(spread_prev, row * out_rows, out_rows, 0)
    power = squares / samples_all
    assoc_score = (
        cross
        * lax.rsqrt(spread_rows + epsilon)[:, None]
        * lax.rsqrt(power + epsilon)[None, :]
        / math.sqrt(samples_all)
    )

    def product(a, b):
        return lax.dot_general(
            a, b, (((0, 2), (0, 2)), ((), ())), preferred_element_type=jnp.float32
        )

    mine = jnp.where(first, upper, other)
    left = product(mine, jnp.where(first, other, upper))
    right = product(mine, jnp.where(first, rest, lower))
    grm_total = grm_prior + jnp.concatenate([left, right], 1) / VARIANTS
    return (grm_total, assoc_score)


def solution(mesh):
    assert mesh.shape["row"] == CORES * mesh.shape["col"]
    in_specs = (
        P("row", "col"),
        P("row", "col"),
        P("row", "col"),
        P("row", None),
        P("row", None),
        P("row", "col"),
    )
    out_specs = (P("row", "col"), P("row", "col"))
    return jax.shard_map(body, mesh=mesh, in_specs=in_specs, out_specs=out_specs, check_vma=False)
```

```python
import math

import jax
import jax.numpy as jnp
from jax import lax
from jax.sharding import PartitionSpec as P

VARIANTS = 4096
epsilon = 1e-05
EVERY = ("row", "col")
CORES = 2


def local_moments(dosage, present):
    values = dosage.astype(jnp.float32)
    weight = present.astype(jnp.float32)
    kept = weight * values
    return jnp.stack([jnp.sum(weight, 0), jnp.sum(kept, 0), jnp.sum(kept * values, 0)])


def summed_over(flat, groups):
    peers = len(groups[0])
    sent = jnp.broadcast_to(flat[None, None], (peers, 1, flat.size))
    arrived = lax.all_to_all(sent, EVERY, 0, 0, tiled=True, axis_index_groups=groups)
    return jnp.sum(arrived, axis=(0, 1))


def finished(moments):
    seen, summed, raw = moments
    observed = jnp.maximum(seen, 1.0)
    centre = summed / observed
    return centre, raw / observed - centre * centre


def half_of(stacked, bit, axis=0):
    return lax.dynamic_index_in_dim(stacked, bit, axis, keepdims=False)


def folded(stacked, bit, pairs):
    return half_of(stacked, bit) + lax.ppermute(half_of(stacked, 1 - bit), EVERY, pairs)


def landing(chips, cols):
    sides, tall, wide = 2, chips // 2, cols // 2
    steps = sorted(range(wide), key=lambda d: min(d, wide - d))
    climbs = sorted(range(tall), key=lambda d: -min(d, tall - d))
    table = []
    for c in range(cols):
        z, low, high, y = c // sides, c % sides, c // wide, c % wide
        targets = [0] * cols
        for step, climb in zip(steps, climbs):
            sources = [half * wide + (y + step) % wide for half in range(2)]
            ends = [(z + climb) % tall * sides + side for side in range(sides)]

            def reach(source, end):
                gap = (source // wide * 2 + low - high * 2 - end % sides) % 4
                return min(gap, 4 - gap)

            straight = [reach(sources[i], ends[i]) for i in range(2)]
            turned = [reach(sources[i], ends[1 - i]) for i in range(2)]
            if max(turned) < max(straight):
                ends = ends[::-1]
            for source, end in zip(sources, ends):
                targets[source] = end
        table.append(targets)
    return table


def body(grm_prior, dosage_now, mask_now, dosage_prev, mask_prev, expression):
    rows, cols = lax.axis_size("row"), lax.axis_size("col")
    chips = rows // CORES
    row, col = lax.axis_index("row"), lax.axis_index("col")
    core = row % CORES
    samples_all = dosage_now.shape[0] * rows
    width = dosage_now.shape[1]
    tested = dosage_prev.shape[1]

    def at(chip, half, column):
        return (chip * CORES + half) * cols + column

    lands = landing(chips, cols)
    blocks = [(k, c) for k in range(chips) for c in range(cols)]

    traits = expression.astype(jnp.float32)
    moments_now = local_moments(dosage_now, mask_now)
    moments_prev = local_moments(dosage_prev, mask_prev)
    squares = jnp.sum(traits * traits, 0)
    swap = [(at(k, h, c), at(k, 1 - h, c)) for k, c in blocks for h in range(CORES)]
    partial = jnp.concatenate([moments_now.reshape(-1), moments_prev.reshape(-1), squares])
    partial = partial + lax.ppermute(partial, EVERY, swap)
    columns = [[at(k, h, c) for k in range(chips)] for c in range(cols) for h in range(CORES)]
    total = summed_over(partial, columns)
    centre_now, spread_now = finished(total[: 3 * width].reshape(3, width))
    centre_prev, spread_prev = finished(
        total[3 * width : 3 * (width + tested)].reshape(3, tested)
    )
    squares = total[3 * (width + tested) :]

    first = core == 0
    weight_now = mask_now.astype(jnp.bfloat16)
    kept_now = weight_now * dosage_now
    pair_now = lax.ppermute(jnp.stack([kept_now, weight_now]), EVERY, swap)

    chip = row // CORES
    level, side = chip // 2, chip % 2
    across = [(at(k, h, c), at(k ^ 1, h, c)) for k, c in blocks for h in range(CORES)]
    genes = expression.shape[1]
    share = genes // 2
    halves = expression.reshape(-1, 2, share)
    weight_prev = mask_prev.astype(jnp.bfloat16)
    tested_raw = [weight_prev * dosage_prev, weight_prev]
    raw = jnp.concatenate([half_of(halves, 1 - side, 1), *tested_raw], 1)
    held = jnp.concatenate([half_of(halves, side, 1), *tested_raw], 1)
    held = jnp.concatenate([held, lax.ppermute(raw, EVERY, across)], 0)
    held = jnp.concatenate([held, lax.ppermute(held, EVERY, swap)], 0)

    def standardized(kept, weight):
        offset = weight.astype(jnp.float32) * (kept.astype(jnp.float32) - centre_now)
        return (offset * lax.rsqrt(spread_now + epsilon)).astype(jnp.bfloat16)

    mine = standardized(kept_now, weight_now)
    partner = standardized(pair_now[0], pair_now[1])
    chip_block = jnp.stack(
        [jnp.where(first, mine, partner), jnp.where(first, partner, mine)]
    )
    mirrored = lax.ppermute(
        chip_block, EVERY, [(at(c, 1, v), at(lands[c][v], 1, c)) for c, v in blocks]
    )
    chip_block = jnp.where(first, chip_block, mirrored)
    genotype = (
        held[:, share + tested :].astype(jnp.float32)
        * (held[:, share : share + tested].astype(jnp.float32) - centre_prev)
    ).astype(jnp.bfloat16)
    layers = chips // 2
    near = layers // 2
    out_rows = tested // rows
    cross = lax.dot_general(
        genotype, held[:, :share], (((0,), (0,)), ((), ())), preferred_element_type=jnp.float32
    ).reshape(layers, 2 * CORES * out_rows, share)
    groups = [[at(k, 0, c) for c in range(cols)] for k in range(chips)] + [
        [at(k, 1, c) for k in lands[c]] for c in range(cols)
    ]
    chip_block, cross = lax.optimization_barrier((chip_block, cross))
    panel = lax.all_to_all(
        jnp.broadcast_to(chip_block[None], (cols, *chip_block.shape)),
        EVERY,
        0,
        0,
        tiled=True,
        axis_index_groups=groups,
    )

    kept = jnp.where(first, 0.0, lax.dynamic_index_in_dim(cross, level, 0, keepdims=False))
    arrivals = []
    for far in range(1, near + 1):
        routes = [(at(k, 0, c), at((k + 2 * far) % chips, 0, c)) for k, c in blocks]
        goal = (level + far) % layers
        if far < near:
            routes += [(at(k, 1, c), at((k - 2 * far) % chips, 1, c)) for k, c in blocks]
            goal = jnp.where(first, goal, (level + layers - far) % layers)
        leaving = lax.dynamic_index_in_dim(cross, goal, 0, keepdims=False)
        arrivals.append(lax.ppermute(leaving, EVERY, routes))

    upper, lower = panel[:, 0], panel[:, 1]
    leaving, kept = lax.optimization_barrier((jnp.where(first, lower, upper), kept))
    other = lax.ppermute(leaving, EVERY, swap)
    rest = lax.ppermute(lower, EVERY, [(at(k, 1, c), at(k, 0, c)) for k, c in blocks])

    total_rows = kept
    for arrived in arrivals:
        total_rows = total_rows + arrived
    shares = total_rows.reshape(2, CORES, out_rows, share)
    own, other_half = half_of(shares, side), lax.ppermute(half_of(shares, 1 - side), EVERY, across)
    left_chip = side == 0
    shares = jnp.concatenate(
        [jnp.where(left_chip, own, other_half), jnp.where(left_chip, other_half, own)], 2
    )
    cross = folded(shares, core, swap)
    spread_rows = lax.dynamic_slice_in_dim(spread_prev, row * out_rows, out_rows, 0)
    power = squares / samples_all
    assoc_score = (
        cross
        * lax.rsqrt(spread_rows + epsilon)[:, None]
        * lax.rsqrt(power + epsilon)[None, :]
        / math.sqrt(samples_all)
    )

    def product(a, b):
        return lax.dot_general(
            a, b, (((0, 2), (0, 2)), ((), ())), preferred_element_type=jnp.float32
        )

    mine = jnp.where(first, upper, other)
    left = product(mine, jnp.where(first, other, upper))
    right = product(mine, jnp.where(first, rest, lower))
    grm_total = grm_prior + jnp.concatenate([left, right], 1) / VARIANTS
    return (grm_total, assoc_score)


def solution(mesh):
    assert mesh.shape["row"] == CORES * mesh.shape["col"]
    in_specs = (
        P("row", "col"),
        P("row", "col"),
        P("row", "col"),
        P("row", None),
        P("row", None),
        P("row", "col"),
    )
    out_specs = (P("row", "col"), P("row", "col"))
    return jax.shard_map(body, mesh=mesh, in_specs=in_specs, out_specs=out_specs, check_vma=False)
```

```python
import math

import jax
import jax.numpy as jnp
from jax import lax
from jax.sharding import PartitionSpec as P

VARIANTS = 4096
epsilon = 1e-05
EVERY = ("row", "col")
CORES = 2


def local_moments(dosage, present):
    values = dosage.astype(jnp.float32)
    weight = present.astype(jnp.float32)
    kept = weight * values
    return jnp.stack([jnp.sum(weight, 0), jnp.sum(kept, 0), jnp.sum(kept * values, 0)])


def summed_over(by_side, groups):
    sent = jnp.concatenate([by_side[:, None]] * (len(groups[0]) // by_side.shape[0]), 0)
    arrived = lax.all_to_all(sent, EVERY, 0, 0, tiled=True, axis_index_groups=groups)
    return jnp.sum(arrived, axis=(0, 1))


def finished(moments):
    seen, summed, raw = moments
    observed = jnp.maximum(seen, 1.0)
    centre = summed / observed
    return centre, raw / observed - centre * centre


def half_of(stacked, bit, axis=0):
    return lax.dynamic_index_in_dim(stacked, bit, axis, keepdims=False)


def folded(stacked, bit, pairs):
    return half_of(stacked, bit) + lax.ppermute(half_of(stacked, 1 - bit), EVERY, pairs)


def landing(chips, cols):
    sides, tall, wide = 2, chips // 2, cols // 2
    steps = sorted(range(wide), key=lambda d: min(d, wide - d))
    climbs = sorted(range(tall), key=lambda d: -min(d, tall - d))
    table = []
    for c in range(cols):
        z, low, high, y = c // sides, c % sides, c // wide, c % wide
        targets = [0] * cols
        for step, climb in zip(steps, climbs):
            sources = [half * wide + (y + step) % wide for half in range(2)]
            ends = [(z + climb) % tall * sides + side for side in range(sides)]

            def reach(source, end):
                gap = (source // wide * 2 + low - high * 2 - end % sides) % 4
                return min(gap, 4 - gap)

            straight = [reach(sources[i], ends[i]) for i in range(2)]
            turned = [reach(sources[i], ends[1 - i]) for i in range(2)]
            if max(turned) < max(straight):
                ends = ends[::-1]
            for source, end in zip(sources, ends):
                targets[source] = end
        table.append(targets)
    return table


def body(grm_prior, dosage_now, mask_now, dosage_prev, mask_prev, expression):
    rows, cols = lax.axis_size("row"), lax.axis_size("col")
    chips = rows // CORES
    row, col = lax.axis_index("row"), lax.axis_index("col")
    core = row % CORES
    samples_all = dosage_now.shape[0] * rows
    width = dosage_now.shape[1]
    tested = dosage_prev.shape[1]

    def at(chip, half, column):
        return (chip * CORES + half) * cols + column

    lands = landing(chips, cols)
    blocks = [(k, c) for k in range(chips) for c in range(cols)]

    traits = expression.astype(jnp.float32)
    moments_now = local_moments(dosage_now, mask_now)
    moments_prev = local_moments(dosage_prev, mask_prev)
    squares = jnp.sum(traits * traits, 0)
    swap = [(at(k, h, c), at(k, 1 - h, c)) for k, c in blocks for h in range(CORES)]
    partial = jnp.concatenate([moments_now.reshape(-1), moments_prev.reshape(-1), squares])
    partial = partial + lax.ppermute(partial, EVERY, swap)
    columns = [[at(k, h, c) for k in range(chips)] for c in range(cols) for h in range(CORES)]
    common, both = partial[: 3 * (width + tested)], partial[3 * (width + tested) :]
    by_side = jnp.stack([jnp.concatenate([common, half]) for half in jnp.split(both, 2)])
    total = summed_over(by_side, columns)
    centre_now, spread_now = finished(total[: 3 * width].reshape(3, width))
    centre_prev, spread_prev = finished(
        total[3 * width : 3 * (width + tested)].reshape(3, tested)
    )
    squares = total[3 * (width + tested) :]

    first = core == 0
    weight_now = mask_now.astype(jnp.bfloat16)
    kept_now = weight_now * dosage_now
    pair_now = lax.ppermute(jnp.stack([kept_now, weight_now]), EVERY, swap)

    chip = row // CORES
    level, side = chip // 2, chip % 2
    across = [(at(k, h, c), at(k ^ 1, h, c)) for k, c in blocks for h in range(CORES)]
    genes = expression.shape[1]
    share = genes // 2
    halves = expression.reshape(-1, 2, share)
    weight_prev = mask_prev.astype(jnp.bfloat16)
    tested_raw = [weight_prev * dosage_prev, weight_prev]
    raw = jnp.concatenate([half_of(halves, 1 - side, 1), *tested_raw], 1)
    held = jnp.concatenate([half_of(halves, side, 1), *tested_raw], 1)
    held = jnp.concatenate([held, lax.ppermute(raw, EVERY, across)], 0)
    held = jnp.concatenate([held, lax.ppermute(held, EVERY, swap)], 0)

    def standardized(kept, weight):
        offset = weight.astype(jnp.float32) * (kept.astype(jnp.float32) - centre_now)
        return (offset * lax.rsqrt(spread_now + epsilon)).astype(jnp.bfloat16)

    mine = standardized(kept_now, weight_now)
    partner = standardized(pair_now[0], pair_now[1])
    chip_block = jnp.stack(
        [jnp.where(first, mine, partner), jnp.where(first, partner, mine)]
    )
    mirrored = lax.ppermute(
        chip_block, EVERY, [(at(c, 1, v), at(lands[c][v], 1, c)) for c, v in blocks]
    )
    chip_block = jnp.where(first, chip_block, mirrored)
    genotype = (
        held[:, share + tested :].astype(jnp.float32)
        * (held[:, share : share + tested].astype(jnp.float32) - centre_prev)
    ).astype(jnp.bfloat16)
    layers = chips // 2
    near = layers // 2
    out_rows = tested // rows
    cross = lax.dot_general(
        genotype, held[:, :share], (((0,), (0,)), ((), ())), preferred_element_type=jnp.float32
    ).reshape(layers, 2 * CORES * out_rows, share)
    groups = [[at(k, 0, c) for c in range(cols)] for k in range(chips)] + [
        [at(k, 1, c) for k in lands[c]] for c in range(cols)
    ]
    chip_block, cross = lax.optimization_barrier((chip_block, cross))
    panel = lax.all_to_all(
        jnp.broadcast_to(chip_block[None], (cols, *chip_block.shape)),
        EVERY,
        0,
        0,
        tiled=True,
        axis_index_groups=groups,
    )

    kept = jnp.where(first, 0.0, lax.dynamic_index_in_dim(cross, level, 0, keepdims=False))
    arrivals = []
    for far in range(1, near + 1):
        routes = [(at(k, 0, c), at((k + 2 * far) % chips, 0, c)) for k, c in blocks]
        goal = (level + far) % layers
        if far < near:
            routes += [(at(k, 1, c), at((k - 2 * far) % chips, 1, c)) for k, c in blocks]
            goal = jnp.where(first, goal, (level + layers - far) % layers)
        leaving = lax.dynamic_index_in_dim(cross, goal, 0, keepdims=False)
        arrivals.append(lax.ppermute(leaving, EVERY, routes))

    upper, lower = panel[:, 0], panel[:, 1]
    leaving, kept = lax.optimization_barrier((jnp.where(first, lower, upper), kept))
    other = lax.ppermute(leaving, EVERY, swap)
    rest = lax.ppermute(lower, EVERY, [(at(k, 1, c), at(k, 0, c)) for k, c in blocks])

    total_rows = kept
    for arrived in arrivals:
        total_rows = total_rows + arrived
    power = squares / samples_all
    total_rows = total_rows * lax.rsqrt(power + epsilon)[None, :]
    shares = total_rows.reshape(2, CORES, out_rows, share)
    own, other_half = half_of(shares, side), lax.ppermute(half_of(shares, 1 - side), EVERY, across)
    left_chip = side == 0
    shares = jnp.concatenate(
        [jnp.where(left_chip, own, other_half), jnp.where(left_chip, other_half, own)], 2
    )
    cross = folded(shares, core, swap)
    spread_rows = lax.dynamic_slice_in_dim(spread_prev, row * out_rows, out_rows, 0)
    assoc_score = cross * lax.rsqrt(spread_rows + epsilon)[:, None] / math.sqrt(samples_all)

    def product(a, b):
        return lax.dot_general(
            a, b, (((0, 2), (0, 2)), ((), ())), preferred_element_type=jnp.float32
        )

    mine = jnp.where(first, upper, other)
    left = product(mine, jnp.where(first, other, upper))
    right = product(mine, jnp.where(first, rest, lower))
    grm_total = grm_prior + jnp.concatenate([left, right], 1) / VARIANTS
    return (grm_total, assoc_score)


def solution(mesh):
    assert mesh.shape["row"] == CORES * mesh.shape["col"]
    in_specs = (
        P("row", "col"),
        P("row", "col"),
        P("row", "col"),
        P("row", None),
        P("row", None),
        P("row", "col"),
    )
    out_specs = (P("row", "col"), P("row", "col"))
    return jax.shard_map(body, mesh=mesh, in_specs=in_specs, out_specs=out_specs, check_vma=False)
```

```python
import math

import jax
import jax.numpy as jnp
from jax import lax
from jax.sharding import PartitionSpec as P

VARIANTS = 4096
epsilon = 1e-05
EVERY = ("row", "col")
CORES = 2


def local_moments(dosage, present):
    values = dosage.astype(jnp.float32)
    weight = present.astype(jnp.float32)
    kept = weight * values
    return jnp.stack([jnp.sum(weight, 0), jnp.sum(kept, 0), jnp.sum(kept * values, 0)])


def summed_over(flat, groups):
    peers = len(groups[0])
    sent = jnp.broadcast_to(flat[None, None], (peers, 1, flat.size))
    arrived = lax.all_to_all(sent, EVERY, 0, 0, tiled=True, axis_index_groups=groups)
    return jnp.sum(arrived, axis=(0, 1))


def finished(moments):
    seen, summed, raw = moments
    observed = jnp.maximum(seen, 1.0)
    centre = summed / observed
    return centre, raw / observed - centre * centre


def half_of(stacked, bit, axis=0):
    return lax.dynamic_index_in_dim(stacked, bit, axis, keepdims=False)


def folded(stacked, bit, pairs):
    return half_of(stacked, bit) + lax.ppermute(half_of(stacked, 1 - bit), EVERY, pairs)


def landing(chips, cols):
    sides, tall, wide = 2, chips // 2, cols // 2
    steps = sorted(range(wide), key=lambda d: min(d, wide - d))
    climbs = sorted(range(tall), key=lambda d: -min(d, tall - d))
    table = []
    for c in range(cols):
        z, low, high, y = c // sides, c % sides, c // wide, c % wide
        targets = [0] * cols
        for step, climb in zip(steps, climbs):
            sources = [half * wide + (y + step) % wide for half in range(2)]
            ends = [(z + climb) % tall * sides + side for side in range(sides)]

            def reach(source, end):
                gap = (source // wide * 2 + low - high * 2 - end % sides) % 4
                return min(gap, 4 - gap)

            straight = [reach(sources[i], ends[i]) for i in range(2)]
            turned = [reach(sources[i], ends[1 - i]) for i in range(2)]
            if max(turned) < max(straight):
                ends = ends[::-1]
            for source, end in zip(sources, ends):
                targets[source] = end
        table.append(targets)
    return table


def body(grm_prior, dosage_now, mask_now, dosage_prev, mask_prev, expression):
    rows, cols = lax.axis_size("row"), lax.axis_size("col")
    chips = rows // CORES
    row, col = lax.axis_index("row"), lax.axis_index("col")
    core = row % CORES
    samples_all = dosage_now.shape[0] * rows
    width = dosage_now.shape[1]
    tested = dosage_prev.shape[1]

    def at(chip, half, column):
        return (chip * CORES + half) * cols + column

    lands = landing(chips, cols)
    blocks = [(k, c) for k in range(chips) for c in range(cols)]

    traits = expression.astype(jnp.float32)
    moments_now = local_moments(dosage_now, mask_now)
    moments_prev = local_moments(dosage_prev, mask_prev)
    squares = jnp.sum(traits * traits, 0)
    swap = [(at(k, h, c), at(k, 1 - h, c)) for k, c in blocks for h in range(CORES)]
    partial = jnp.concatenate([moments_now.reshape(-1), moments_prev.reshape(-1), squares])
    partial = partial + lax.ppermute(partial, EVERY, swap)
    columns = [[at(k, h, c) for k in range(chips)] for c in range(cols) for h in range(CORES)]
    total = summed_over(partial, columns)
    centre_now, spread_now = finished(total[: 3 * width].reshape(3, width))
    centre_prev, spread_prev = finished(
        total[3 * width : 3 * (width + tested)].reshape(3, tested)
    )
    squares = total[3 * (width + tested) :]

    first = core == 0
    weight_now = mask_now.astype(jnp.bfloat16)
    kept_now = weight_now * dosage_now
    pair_now = lax.ppermute(jnp.stack([kept_now, weight_now]), EVERY, swap)

    chip = row // CORES
    level, side = chip // 2, chip % 2
    across = [(at(k, h, c), at(k ^ 1, h, c)) for k, c in blocks for h in range(CORES)]
    genes = expression.shape[1]
    share = genes // 2
    halves = expression.reshape(-1, 2, share)
    weight_prev = mask_prev.astype(jnp.bfloat16)
    tested_raw = [weight_prev * dosage_prev, weight_prev]
    raw = jnp.concatenate([half_of(halves, 1 - side, 1), *tested_raw], 1)
    held = jnp.concatenate([half_of(halves, side, 1), *tested_raw], 1)
    held = jnp.concatenate([held, lax.ppermute(raw, EVERY, across)], 0)
    held = jnp.concatenate([held, lax.ppermute(held, EVERY, swap)], 0)

    def standardized(kept, weight):
        offset = weight.astype(jnp.float32) * (kept.astype(jnp.float32) - centre_now)
        return (offset * lax.rsqrt(spread_now + epsilon)).astype(jnp.bfloat16)

    mine = standardized(kept_now, weight_now)
    partner = standardized(pair_now[0], pair_now[1])
    chip_block = jnp.stack(
        [jnp.where(first, mine, partner), jnp.where(first, partner, mine)]
    )
    mirrored = lax.ppermute(
        chip_block, EVERY, [(at(c, 1, v), at(lands[c][v], 1, c)) for c, v in blocks]
    )
    chip_block = jnp.where(first, chip_block, mirrored)
    genotype = (
        held[:, share + tested :].astype(jnp.float32)
        * (held[:, share : share + tested].astype(jnp.float32) - centre_prev)
    ).astype(jnp.bfloat16)
    layers = chips // 2
    near = layers // 2
    out_rows = tested // rows
    cross = lax.dot_general(
        genotype, held[:, :share], (((0,), (0,)), ((), ())), preferred_element_type=jnp.float32
    ).reshape(layers, 2 * CORES * out_rows, share)
    groups = [[at(k, 0, c) for c in range(cols)] for k in range(chips)] + [
        [at(k, 1, c) for k in lands[c]] for c in range(cols)
    ]
    chip_block, cross = lax.optimization_barrier((chip_block, cross))
    panel = lax.all_to_all(
        jnp.broadcast_to(chip_block[None], (cols, *chip_block.shape)),
        EVERY,
        0,
        0,
        tiled=True,
        axis_index_groups=groups,
    )

    kept = jnp.where(first, 0.0, lax.dynamic_index_in_dim(cross, level, 0, keepdims=False))
    arrivals = []
    for far in range(1, near + 1):
        routes = [(at(k, 0, c), at((k + 2 * far) % chips, 0, c)) for k, c in blocks]
        goal = (level + far) % layers
        if far < near:
            routes += [(at(k, 1, c), at((k - 2 * far) % chips, 1, c)) for k, c in blocks]
            goal = jnp.where(first, goal, (level + layers - far) % layers)
        leaving = lax.dynamic_index_in_dim(cross, goal, 0, keepdims=False)
        arrivals.append(lax.ppermute(leaving, EVERY, routes))

    upper, lower = panel[:, 0], panel[:, 1]
    leaving, kept = lax.optimization_barrier((jnp.where(first, lower, upper), kept))
    other = lax.ppermute(leaving, EVERY, swap)
    rest = lax.ppermute(lower, EVERY, [(at(k, 1, c), at(k, 0, c)) for k, c in blocks])

    total_rows = kept
    for arrived in arrivals:
        total_rows = total_rows + arrived
    power = jnp.where(side == 0, squares[:share], squares[share:]) / samples_all
    total_rows = total_rows * lax.rsqrt(power + epsilon)[None, :]
    shares = total_rows.reshape(2, CORES, out_rows, share)
    own, other_half = half_of(shares, side), lax.ppermute(half_of(shares, 1 - side), EVERY, across)
    left_chip = side == 0
    shares = jnp.concatenate(
        [jnp.where(left_chip, own, other_half), jnp.where(left_chip, other_half, own)], 2
    )
    cross = folded(shares, core, swap)
    spread_rows = lax.dynamic_slice_in_dim(spread_prev, row * out_rows, out_rows, 0)
    assoc_score = cross * lax.rsqrt(spread_rows + epsilon)[:, None] / math.sqrt(samples_all)

    def product(a, b):
        return lax.dot_general(
            a, b, (((0, 2), (0, 2)), ((), ())), preferred_element_type=jnp.float32
        )

    mine = jnp.where(first, upper, other)
    left = product(mine, jnp.where(first, other, upper))
    right = product(mine, jnp.where(first, rest, lower))
    grm_total = grm_prior + jnp.concatenate([left, right], 1) / VARIANTS
    return (grm_total, assoc_score)


def solution(mesh):
    assert mesh.shape["row"] == CORES * mesh.shape["col"]
    in_specs = (
        P("row", "col"),
        P("row", "col"),
        P("row", "col"),
        P("row", None),
        P("row", None),
        P("row", "col"),
    )
    out_specs = (P("row", "col"), P("row", "col"))
    return jax.shard_map(body, mesh=mesh, in_specs=in_specs, out_specs=out_specs, check_vma=False)
```
